256 devices in a mesh: depth: 32 (over x, z_lo, y), cols: 8 (over z_hi, core).
Axes of the slice: x: 4, y: 4, z: 8 (z_hi: 4, z_lo: 2; z = z_hi * 2 + z_lo), core: 2. Of those that a mesh axis runs over, the one named last changes fastest.
Arguments:
- amplitudes: float32 [2304, 32768], P('cols', 'depth'), may hold values from -6 to 6
- integrals: float32 [32768, 8192], P('depth', 'cols'), may hold values from -0.03125 to 0.03125
- residual_in: float32 [2304, 8192], P('depth', 'cols'), may hold values from -4 to 4
Outputs:
- residual_out: float32 [2304, 8192], P('depth', 'cols')
The draws below stay inside these ranges and needn't reach their ends.
All inputs are finite; a program needn't handle non-finite values.
Results may differ from the reference program's by a relative error of at most 0.000071.
Values sent between devices are 32-bit elements; how exact they have to be, the bound alone decides.
A program may use at most 64 MiB of HBM per device.

```python
import jax
import jax.numpy as jnp
from jax import lax

IJ = 2304
CD = 32768
AB = 8192


def strengthened(result, own_key, source, target, shards_of, factor):
    def block_of(position):
        return (jnp.arange(result.shape[position]) // (result.shape[position] // shards_of)).reshape((-1,) + (1,) * (result.ndim - 1 - position))

    near = jax.random.permutation(own_key, shards_of)[block_of(target)]
    other_side = (block_of(target) + shards_of // 2) % shards_of
    return jnp.where((block_of(source) == near) | (block_of(source) == other_side), factor * result, result)


def block_levels(rng, extent, pieces, low, high):
    level, own = 1.0, jax.random.fold_in(rng, 6)
    for axis_at, parts in pieces:
        heights = jnp.exp(jax.random.uniform(jax.random.fold_in(own, axis_at), (parts,), jnp.float32, low / len(pieces), high / len(pieces)))
        level = level * jnp.repeat(heights, extent[axis_at] // parts).reshape([-1 if axis == axis_at else 1 for axis in range(len(extent))])
    return level


def noise(key, extent, deviation, reach, split=(), held_as=jnp.bfloat16):
    drawn = jax.random.normal(key, extent, jnp.float32) * deviation
    if len(split) > 0:
        drawn = block_levels(key, extent, split, -0.22, 0.18) * drawn
    return jnp.clip(drawn, min=-reach, max=reach).astype(held_as)


def heavy_noise(stream_key, dims, spread, bound, pieces, heavy, dtype=jnp.bfloat16):
    entries = spread * jax.random.normal(stream_key, dims, jnp.float32)
    if pieces:
        entries = entries * block_levels(stream_key, dims, pieces, -0.22, 0.18)
    return jnp.clip(strengthened(entries, jax.random.fold_in(stream_key, 3), *heavy), -bound, bound).astype(dtype)


def setup_inputs(seed: int = 0) -> dict:
    seeds = jax.random.split(jax.random.key(seed), 4)
    amplitudes = heavy_noise(seeds[0], (IJ, CD), 1.0, 6.0, ((0, 8), (1, 32)), (1, 0, 32, 2.75), jnp.float32)
    integrals = noise(seeds[1], (CD, AB), CD ** -0.5, 0.03125, ((0, 32), (1, 8)), jnp.float32)
    residual_in = noise(seeds[2], (IJ, AB), 0.5, 4.0, ((0, 32), (1, 8)), jnp.float32)
    return {"amplitudes": amplitudes, "integrals": integrals, "residual_in": residual_in}


def reference(amplitudes, integrals, residual_in):
    ladder = jnp.dot(amplitudes, integrals, precision=lax.Precision.HIGHEST, preferred_element_type=jnp.float32)
    return residual_in + ladder
```

```python
import functools

import jax
import jax.numpy as jnp
from jax import lax
from jax.experimental import pallas as pl
from jax.experimental.pallas import tpu as pltpu
from jax.sharding import PartitionSpec as P

MESH = pl.DeviceIdType.MESH
R = 8
T = 72 // R
AHEAD = 2
K = 1024
NB = 512
PIECES = 4
HOPS = (1, -1, 2)


def kernel(a_ref, b_ref, o_ref, apan, bown, bsib, bh, bl, p1, p2, r1, r2, q1, q2, s1, s2, red, zr,
           own_sem, bown_sem, bs_sem, br_sem, ags, agr, fws, fwr, st1s, st1r, st2s, st2r, zs, zrs):
    d = lax.axis_index("depth")
    j = lax.axis_index("cols")
    x, zl, y = d // 8, (d // 4) % 2, d % 4
    zh, c = j // 2, j % 2

    def dev(x_, zl_, y_, zh_, c_):
        return (x_ * 8 + zl_ * 4 + y_, zh_ * 2 + c_)

    def ring(v, n):
        return (v + n + 4) % 4

    up = dev(x, zl, y, ring(zh, 1), c)
    down = dev(x, zl, y, ring(zh, -1), c)
    sib = dev(x, zl, y, zh, 1 - c)
    xs = [dev(ring(x, n), zl, y, zh, c) for n in HOPS]
    ys = [dev(x, zl, ring(y, n), zh, c) for n in HOPS]
    far = [dev(x, 1 - zl, y, zh, h) for h in range(2)]
    opp = ring(zh, 2)

    def rcopy(src, dst, ss, rs, to):
        return pltpu.make_async_remote_copy(
            src_ref=src, dst_ref=dst, send_sem=ss, recv_sem=rs, device_id=to, device_id_type=MESH
        )

    def own_copy(s):
        return pltpu.make_async_copy(a_ref.at[:, s], apan.at[s, zh], own_sem.at[s])

    bcopy = pltpu.make_async_copy(b_ref, bown, bown_sem)
    bcopy.start()

    peers = [up, down, sib] + xs + ys + far
    barrier = pltpu.get_barrier_semaphore()
    for peer in peers:
        pl.semaphore_signal(barrier, inc=1, device_id=peer, device_id_type=MESH)
    pl.semaphore_wait(barrier, len(peers))

    def ag(s, way):
        return rcopy(a_ref.at[:, s], apan.at[s, zh], ags.at[way, s], agr.at[way, s], (up, down)[way])

    def ag_in(s, way):
        blk = ring(zh, (-1, 1)[way])
        return rcopy(apan.at[s, blk], apan.at[s, blk], ags.at[way, s], agr.at[way, s], (up, down)[way])

    def fw(s, way):
        blk = ring(zh, (-1, 1)[way])
        part = pl.ds(2 * way, 2)
        return rcopy(apan.at[s, blk, part], apan.at[s, blk, part], fws.at[way, s], fwr.at[way, s],
                     (up, down)[way])

    def fw_in(s, way):
        part = pl.ds(2 * way, 2)
        return rcopy(apan.at[s, opp, part], apan.at[s, opp, part], fws.at[way, s], fwr.at[way, s],
                     (up, down)[way])

    def bs(i):
        rows = pl.ds(i * (K // PIECES), K // PIECES)
        return rcopy(b_ref.at[rows], bsib.at[rows], bs_sem.at[i], br_sem.at[i], sib)

    def st1(s, path, i):
        if path == 0:
            return rcopy(p1.at[s, ring(x, HOPS[i])], r1.at[s, i], st1s.at[0, i, s], st1r.at[0, i, s], xs[i])
        return rcopy(p2.at[s, :, ring(y, HOPS[i])], r2.at[s, i], st1s.at[1, i, s], st1r.at[1, i, s], ys[i])

    def st2(s, path, i):
        if path == 0:
            return rcopy(q1.at[s, ring(y, HOPS[i])], s1.at[s, i], st2s.at[0, i, s], st2r.at[0, i, s], ys[i])
        return rcopy(q2.at[s, ring(x, HOPS[i])], s2.at[s, i], st2s.at[1, i, s], st2r.at[1, i, s], xs[i])

    def zfar(s, h):
        return rcopy(red.at[h, s], zr.at[0, s], zs.at[h, s], zrs.at[0, s], far[h])

    def zsib(s):
        return rcopy(red.at[1 - c, s], zr.at[1, s], zs.at[0, s], zrs.at[1, s], sib)

    def zin(s, k):
        return rcopy(red.at[0, s], zr.at[k, s], zs.at[0, s], zrs.at[k, s], sib)

    for s in range(AHEAD):
        for way in range(2):
            ag(s, way).start()
    for i in range(PIECES):
        bs(i).start()

    @pl.loop(0, T)
    def _(s):
        own_copy(s).start()

    def split(src, i, half):
        rows = pl.ds(pl.multiple_of(i * 128, 128), 128)
        v = src[rows, :]
        hi = v.astype(jnp.bfloat16)
        lo = (v - hi.astype(jnp.float32)).astype(jnp.bfloat16)
        cols = pl.ds(pl.multiple_of(half * K, K), K)
        bh[rows, cols] = hi
        bl[rows, cols] = lo

    def pass_on(s):
        for way in range(2):
            ag_in(s, way).wait_recv()
            fw(s, way).start()

    pass_on(0)
    bcopy.wait()

    @pl.loop(0, K // 128)
    def _(i):
        split(bown, i, c)

    for i in range(PIECES):
        bs(i).wait_recv()

    @pl.loop(0, K // 128)
    def _(i):
        split(bsib, i, 1 - c)

    def multiply(s):
        a = apan[s].reshape(16 * R, K)
        hi = a.astype(jnp.bfloat16)
        lo = (a - hi.astype(jnp.float32)).astype(jnp.bfloat16)
        both = jnp.concatenate([hi, lo], axis=0)
        for n in range(2 * K // NB):
            cols = pl.ds(n * NB, NB)
            two = jnp.dot(both, bh[:, cols], preferred_element_type=jnp.float32)
            acc = jnp.dot(hi, bl[:, cols], preferred_element_type=jnp.float32)
            acc = (two[: 16 * R] + (two[16 * R :] + acc)).reshape(4, 4, R, NB)
            if n * NB < K:
                p1[s, :, :, :, n * NB : (n + 1) * NB] = acc
            else:
                p2[s, :, :, :, n * NB - K : (n + 1) * NB - K] = acc

    @pl.loop(0, T + 3)
    def _(s):
        @pl.when(s + AHEAD < T)
        def _():
            for way in range(2):
                ag(s + AHEAD, way).start()

        @pl.when(s + 1 < T)
        def _():
            pass_on(s + 1)

        @pl.when(s < T)
        def _():
            own_copy(s).wait()
            for way in range(2):
                fw_in(s, way).wait_recv()
            multiply(s)
            for i in range(3):
                for path in range(2):
                    st1(s, path, i).start()

        @pl.when((s >= 1) & (s < T + 1))
        def _():
            t = s - 1
            for path in range(2):
                for i in range(3):
                    st1(t, path, i).wait_recv()
            q1[t] = (p1[t, x] + r1[t, 0]) + (r1[t, 1] + r1[t, 2])
            q2[t] = (p2[t, :, y] + r2[t, 0]) + (r2[t, 1] + r2[t, 2])
            for i in range(3):
                for path in range(2):
                    st2(t, path, i).start()

        @pl.when((s >= 2) & (s < T + 2))
        def _():
            t = s - 2
            for path in range(2):
                for i in range(3):
                    st2(t, path, i).wait_recv()
            red[0, t] = (q1[t, y] + s1[t, 0]) + (s1[t, 1] + s1[t, 2])
            red[1, t] = (q2[t, x] + s2[t, 0]) + (s2[t, 1] + s2[t, 2])

            @pl.when(zl == c)
            def _():
                zsib(t).start()

            @pl.when(zl != c)
            def _():
                for h in range(2):
                    zfar(t, h).start()

        @pl.when(s >= 3)
        def _():
            t = s - 3
            zin(t, 0).wait_recv()

            @pl.when(zl == c)
            def _():
                o_ref[t] = red[c, t] + zr[0, t]

            @pl.when(zl != c)
            def _():
                zin(t, 1).wait_recv()
                o_ref[t] = zr[0, t] + zr[1, t]

    for i in range(PIECES):
        bs(i).wait_send()

    @pl.loop(0, T)
    def _(s):
        for way in range(2):
            ag(s, way).wait_send()
            fw(s, way).wait_send()
        for path in range(2):
            for i in range(3):
                st1(s, path, i).wait_send()
                st2(s, path, i).wait_send()

        @pl.when(zl == c)
        def _():
            zsib(s).wait_send()

        @pl.when(zl != c)
        def _():
            for h in range(2):
                zfar(s, h).wait_send()


def ladder(a, b):
    f32, bf16 = jnp.float32, jnp.bfloat16
    dma = pltpu.SemaphoreType.DMA
    return pl.pallas_call(
        kernel,
        out_shape=jax.ShapeDtypeStruct((T, R, K), f32),
        in_specs=[pl.BlockSpec(memory_space=pl.ANY)] * 2,
        out_specs=pl.BlockSpec(memory_space=pltpu.VMEM),
        scratch_shapes=[
            pltpu.VMEM((T, 4, 4, R, K), f32),
            pltpu.VMEM((K, K), f32),
            pltpu.VMEM((K, K), f32),
            pltpu.VMEM((K, 2 * K), bf16),
            pltpu.VMEM((K, 2 * K), bf16),
            pltpu.VMEM((T, 4, 4, R, K), f32),
            pltpu.VMEM((T, 4, 4, R, K), f32),
            pltpu.VMEM((T, 3, 4, R, K), f32),
            pltpu.VMEM((T, 3, 4, R, K), f32),
            pltpu.VMEM((T, 4, R, K), f32),
            pltpu.VMEM((T, 4, R, K), f32),
            pltpu.VMEM((T, 3, R, K), f32),
            pltpu.VMEM((T, 3, R, K), f32),
            pltpu.VMEM((2, T, R, K), f32),
            pltpu.VMEM((2, T, R, K), f32),
            dma((T,)), dma, dma((PIECES,)), dma((PIECES,)),
            dma((2, T)), dma((2, T)), dma((2, T)), dma((2, T)),
            dma((2, 3, T)), dma((2, 3, T)), dma((2, 3, T)), dma((2, 3, T)),
            dma((2, T)), dma((2, T)),
        ],
        cost_estimate=pl.CostEstimate(flops=2 * 1152 * 2048 * 1024 * 3, bytes_accessed=8 * 2**20, transcendentals=0),
        compiler_params=pltpu.CompilerParams(collective_id=0, has_side_effects=True, vmem_limit_bytes=60 * 2**20),
    )(a, b)


def shards(amplitudes, integrals, residual_in):
    owned = ladder(amplitudes.reshape(4, T, R, K), integrals)
    return residual_in + owned.reshape(72, K)


def solution(mesh):
    placed = (P("cols", "depth"), P("depth", "cols"), P("depth", "cols"))
    return jax.shard_map(
        shards, mesh=mesh, in_specs=placed, out_specs=P("depth", "cols"), check_vma=False
    )
```

```python
import jax
import jax.numpy as jnp
from jax import lax
from jax.experimental import pallas as pl
from jax.experimental.pallas import tpu as pltpu
from jax.sharding import PartitionSpec as P

MESH = pl.DeviceIdType.MESH
K = 1024
R = 8
T = 72 // R
AHEAD = 2
UN = 2
W = K // UN
U = T * UN
LAG = 2
HELD = (T - 1) * UN - 3 * LAG
PIECES = 4
HOPS = (1, -1, 2)


def kernel(a_ref, b_ref, o_ref, apan, bown, bsib, bh, bl, both, p, ra, rbc, m, q, r2, red, zr,
           own_sem, bown_sem, bss, bsr, ags, agr, fws, fwr, as_, ar, bs_, cs, bcr, st2s, st2r, zs, zrs):
    d = lax.axis_index("depth")
    j = lax.axis_index("cols")
    x, zl, y = d // 8, (d // 4) % 2, d % 4
    zh, c = j // 2, j % 2

    def dev(x_, zl_, y_, zh_, c_):
        return (x_ * 8 + zl_ * 4 + y_, zh_ * 2 + c_)

    def ring(v, n):
        return (v + n + 4) % 4

    up = dev(x, zl, y, ring(zh, 1), c)
    down = dev(x, zl, y, ring(zh, -1), c)
    sib = dev(x, zl, y, zh, 1 - c)
    xs = [dev(ring(x, n), zl, y, zh, c) for n in HOPS]
    ys = [dev(x, zl, ring(y, n), zh, c) for n in HOPS]
    far = [dev(x, 1 - zl, y, zh, h) for h in range(2)]
    opp = ring(zh, 2)
    first, second = (xs, ys), (ys, xs)
    at1, at2 = (x, y), (y, x)

    def rcopy(src, dst, ss, rs, to):
        return pltpu.make_async_remote_copy(
            src_ref=src, dst_ref=dst, send_sem=ss, recv_sem=rs, device_id=to, device_id_type=MESH
        )

    def own_copy(s):
        return pltpu.make_async_copy(a_ref.at[:, s], apan.at[s, zh], own_sem.at[s])

    bcopy = pltpu.make_async_copy(b_ref, bown, bown_sem)
    bcopy.start()

    peers = [up, down, sib] + xs + ys + far
    barrier = pltpu.get_barrier_semaphore()
    for peer in peers:
        pl.semaphore_signal(barrier, inc=1, device_id=peer, device_id_type=MESH)
    pl.semaphore_wait(barrier, len(peers))

    def ag(s, way):
        return rcopy(a_ref.at[:, s], apan.at[s, zh], ags.at[way], agr.at[way, s], (up, down)[way])

    def ag_in(s, way):
        blk = ring(zh, (-1, 1)[way])
        return rcopy(apan.at[s, blk], apan.at[s, blk], ags.at[way], agr.at[way, s], (up, down)[way])

    def fw(s, way):
        blk = ring(zh, (-1, 1)[way])
        part = pl.ds(2 * way, 2)
        return rcopy(apan.at[s, blk, part], apan.at[s, blk, part], fws.at[way], fwr.at[s],
                     (up, down)[way])

    def fw_in(s):
        return rcopy(apan.at[s, opp], apan.at[s, opp], fws.at[0], fwr.at[s], up)

    def bs(i):
        rows = pl.ds(i * (K // PIECES), K // PIECES)
        return rcopy(b_ref.at[rows], bsib.at[rows], bss, bsr.at[i], sib)

    def send_a(u, k, w):
        return rcopy(p.at[u, k, ring(at1[k], 2), pl.ds(2 * w, 2)], ra.at[u, k, w], as_, ar.at[u], first[k][w])

    def send_b(u, k, w):
        return rcopy(p.at[u, k, ring(at1[k], HOPS[w]), pl.ds(2 - 2 * w, 2)], rbc.at[u, 0, k, w], bs_, bcr.at[u],
                     first[k][w])

    def send_c(u, k, w):
        return rcopy(m.at[u, k, w], rbc.at[u, 1, k, w], cs, bcr.at[u], first[k][w])

    def send_2(u, k, i):
        return rcopy(q.at[u, k, ring(at2[k], HOPS[i])], r2.at[u, k, i], st2s, st2r.at[u], second[k][i])

    def arrived(buf, sem):
        rcopy(buf, buf, ags.at[0], sem, up).wait_recv()

    def sent(buf, sem):
        rcopy(buf, buf, sem, agr.at[0, 0], up).wait_send()

    def zfar(u, h):
        return rcopy(red.at[u, h], zr.at[u, 0], zs, zrs.at[u], far[h])

    def zsib(u):
        return rcopy(red.at[u, 1 - c], zr.at[u, 1], zs, zrs.at[u], sib)

    PAIRS = [(k, w) for w in range(2) for k in range(2)]

    for s in range(AHEAD):
        for way in range(2):
            ag(s, way).start()
    for i in range(PIECES):
        bs(i).start()

    @pl.loop(0, T)
    def _(s):
        own_copy(s).start()

    def split(src, i, half):
        rows = pl.ds(pl.multiple_of(i * 128, 128), 128)
        v = src[rows, :]
        hi = v.astype(jnp.bfloat16)
        lo = (v - hi.astype(jnp.float32)).astype(jnp.bfloat16)
        cols = pl.ds(pl.multiple_of(half * K, K), K)
        bh[rows, cols] = hi
        bl[rows, cols] = lo

    def pass_on(s):
        for way in range(2):
            ag_in(s, way).wait_recv()
            fw(s, way).start()

    bcopy.wait()

    @pl.loop(0, K // 128)
    def _(i):
        split(bown, i, c)

    pass_on(0)

    for i in range(PIECES):
        bs(i).wait_recv()

    @pl.loop(0, K // 128)
    def _(i):
        split(bsib, i, 1 - c)

    def split_rows(s):
        a = apan[s].reshape(16 * R, K)
        hi = a.astype(jnp.bfloat16)
        both[: 16 * R] = hi
        both[16 * R :] = (a - hi.astype(jnp.float32)).astype(jnp.bfloat16)

    def multiply(u, i):
        for half in range(2):
            cols = pl.ds(pl.multiple_of(half * K + i * W, W), W)
            two = jnp.dot(both[...], bh[:, cols], preferred_element_type=jnp.float32)
            acc = jnp.dot(both[: 16 * R], bl[:, cols], preferred_element_type=jnp.float32)
            acc = (two[: 16 * R] + (two[16 * R :] + acc)).reshape(4, 4, R, W)
            if half == 0:
                p[u, 0] = acc
            else:
                for n in range(4):
                    p[u, 1, :, n] = acc[n]

    def exchange(u):
        @pl.when(zl == c)
        def _():
            zsib(u).start()

        @pl.when(zl != c)
        def _():
            for h in range(2):
                zfar(u, h).start()

    def finish(u):
        cols = pl.ds(pl.multiple_of((u % UN) * W, W), W)

        @pl.when(zl == c)
        def _():
            arrived(zr.at[u, 0], zrs.at[u])
            o_ref[u // UN, :, cols] = red[u, c] + zr[u, 0]

        @pl.when(zl != c)
        def _():
            arrived(zr.at[u], zrs.at[u])
            o_ref[u // UN, :, cols] = zr[u, 0] + zr[u, 1]

    @pl.loop(0, U + 4 * LAG)
    def _(u):
        i = u % UN
        s = u // UN

        @pl.when((i == 0) & (s < T))
        def _():
            @pl.when(s + AHEAD < T)
            def _():
                for way in range(2):
                    ag(s + AHEAD, way).start()

            @pl.when(s + 1 < T)
            def _():
                pass_on(s + 1)

            own_copy(s).wait()
            fw_in(s).wait_recv()
            split_rows(s)

        @pl.when(u == (T - 1) * UN)
        def _():
            @pl.loop(0, HELD)
            def _(t):
                exchange(t)

        @pl.when(u < U)
        def _():
            multiply(u, i)
            for k, w in PAIRS:
                send_a(u, k, w).start()
            for k, w in PAIRS:
                send_b(u, k, w).start()

        @pl.when((u >= LAG) & (u < U + LAG))
        def _():
            t = u - LAG
            arrived(ra.at[t], ar.at[t])
            for k, w in PAIRS:
                m[t, k, w] = p[t, k, ring(at1[k], HOPS[w]), 2 * w : 2 * w + 2] + ra[t, k, w]
                send_c(t, k, w).start()

        @pl.when((u >= 2 * LAG) & (u < U + 2 * LAG))
        def _():
            t = u - 2 * LAG
            arrived(rbc.at[t], bcr.at[t])
            for k in range(2):
                for w in range(2):
                    part = slice(2 * w, 2 * w + 2)
                    q[t, k, part] = p[t, k, at1[k], part] + (rbc[t, 0, k, 1 - w] + rbc[t, 1, k, w])
                for i2 in range(3):
                    send_2(t, k, i2).start()

        @pl.when(u == U - 1 + 2 * LAG)
        def _():
            @pl.loop(0, HELD)
            def _(t):
                finish(t)

        @pl.when((u >= 3 * LAG) & (u < U + 3 * LAG))
        def _():
            t = u - 3 * LAG
            arrived(r2.at[t], st2r.at[t])
            for k in range(2):
                red[t, k] = (q[t, k, at2[k]] + r2[t, k, 0]) + (r2[t, k, 1] + r2[t, k, 2])

            @pl.when(t >= HELD)
            def _():
                exchange(t)

        @pl.when(u >= HELD + 4 * LAG)
        def _():
            finish(u - 4 * LAG)

    sent(bsib, bss)
    for way in range(2):
        sent(apan.at[:, 0], ags.at[way])
        sent(apan.at[:, 0, pl.ds(0, 2)], fws.at[way])
    sent(ra, as_)
    sent(rbc.at[:, 0], bs_)
    sent(m, cs)
    sent(r2, st2s)

    @pl.when(zl == c)
    def _():
        sent(red.at[:, 0], zs)

    @pl.when(zl != c)
    def _():
        sent(red, zs)


def ladder(a, b):
    f32, bf16 = jnp.float32, jnp.bfloat16
    dma = pltpu.SemaphoreType.DMA
    return pl.pallas_call(
        kernel,
        out_shape=jax.ShapeDtypeStruct((T, R, K), f32),
        in_specs=[pl.BlockSpec(memory_space=pl.ANY)] * 2,
        out_specs=pl.BlockSpec(memory_space=pltpu.VMEM),
        scratch_shapes=[
            pltpu.VMEM((T, 4, 4, R, K), f32),
            pltpu.VMEM((K, K), f32),
            pltpu.VMEM((K, K), f32),
            pltpu.VMEM((K, 2 * K), bf16),
            pltpu.VMEM((K, 2 * K), bf16),
            pltpu.VMEM((32 * R, K), bf16),
            pltpu.VMEM((U, 2, 4, 4, R, W), f32),
            pltpu.VMEM((U, 2, 2, 2, R, W), f32),
            pltpu.VMEM((U, 2, 2, 2, 2, R, W), f32),
            pltpu.VMEM((U, 2, 2, 2, R, W), f32),
            pltpu.VMEM((U, 2, 4, R, W), f32),
            pltpu.VMEM((U, 2, 3, R, W), f32),
            pltpu.VMEM((U, 2, R, W), f32),
            pltpu.VMEM((U, 2, R, W), f32),
            dma((T,)), dma, dma, dma((PIECES,)),
            dma((2,)), dma((2, T)), dma((2,)), dma((T,)),
            dma, dma((U,)), dma, dma, dma((U,)), dma, dma((U,)), dma, dma((U,)),
        ],
        cost_estimate=pl.CostEstimate(flops=2 * 1152 * 2048 * 1024 * 3, bytes_accessed=8 * 2**20, transcendentals=0),
        compiler_params=pltpu.CompilerParams(collective_id=0, has_side_effects=True, vmem_limit_bytes=52 * 2**20),
    )(a, b)


def shards(amplitudes, integrals, residual_in):
    owned = ladder(amplitudes.reshape(4, T, R, K), integrals)
    return residual_in + owned.reshape(72, K)


def solution(mesh):
    placed = (P("cols", "depth"), P("depth", "cols"), P("depth", "cols"))
    return jax.shard_map(
        shards, mesh=mesh, in_specs=placed, out_specs=P("depth", "cols"), check_vma=False
    )
```

```python
import jax
import jax.numpy as jnp
from jax import lax
from jax.experimental import pallas as pl
from jax.experimental.pallas import tpu as pltpu
from jax.sharding import PartitionSpec as P

MESH = pl.DeviceIdType.MESH
K = 1024
R = 8
T = 72 // R
AHEAD = 2
UN = 2
W = K // UN
U = T * UN
LAG = 2
HELD = 4
PIECES = 4
HOPS = (1, -1, 2)


def kernel(a_ref, b_ref, o_ref, apan, bown, bsib, bh, bl, both, p, ra, rbc, m, q, r2, red, zr,
           own_sem, bown_sem, bss, bsr, ags, agr, fws, fwr, as_, ar, bs_, cs, bcr, st2s, st2r, zs, zrs):
    d = lax.axis_index("depth")
    j = lax.axis_index("cols")
    x, zl, y = d // 8, (d // 4) % 2, d % 4
    zh, c = j // 2, j % 2

    def dev(x_, zl_, y_, zh_, c_):
        return (x_ * 8 + zl_ * 4 + y_, zh_ * 2 + c_)

    def ring(v, n):
        return (v + n + 4) % 4

    up = dev(x, zl, y, ring(zh, 1), c)
    down = dev(x, zl, y, ring(zh, -1), c)
    sib = dev(x, zl, y, zh, 1 - c)
    xs = [dev(ring(x, n), zl, y, zh, c) for n in HOPS]
    ys = [dev(x, zl, ring(y, n), zh, c) for n in HOPS]
    far = [dev(x, 1 - zl, y, zh, h) for h in range(2)]
    opp = ring(zh, 2)
    first, second = (xs, ys), (ys, xs)
    at1, at2 = (x, y), (y, x)

    def rcopy(src, dst, ss, rs, to):
        return pltpu.make_async_remote_copy(
            src_ref=src, dst_ref=dst, send_sem=ss, recv_sem=rs, device_id=to, device_id_type=MESH
        )

    def own_copy(s):
        return pltpu.make_async_copy(a_ref.at[:, s], apan.at[s, zh], own_sem.at[s])

    bcopy = pltpu.make_async_copy(b_ref, bown, bown_sem)
    bcopy.start()

    peers = [up, down, sib] + xs + ys + far
    barrier = pltpu.get_barrier_semaphore()
    for peer in peers:
        pl.semaphore_signal(barrier, inc=1, device_id=peer, device_id_type=MESH)
    pl.semaphore_wait(barrier, len(peers))

    def ag(s, way):
        return rcopy(a_ref.at[:, s], apan.at[s, zh], ags.at[way], agr.at[way, s], (up, down)[way])

    def ag_in(s, way):
        blk = ring(zh, (-1, 1)[way])
        return rcopy(apan.at[s, blk], apan.at[s, blk], ags.at[way], agr.at[way, s], (up, down)[way])

    def fw(s, way):
        blk = ring(zh, (-1, 1)[way])
        part = pl.ds(2 * way, 2)
        return rcopy(apan.at[s, blk, part], apan.at[s, blk, part], fws.at[way], fwr.at[s],
                     (up, down)[way])

    def fw_in(s):
        return rcopy(apan.at[s, opp], apan.at[s, opp], fws.at[0], fwr.at[s], up)

    def bs(i):
        rows = pl.ds(i * (K // PIECES), K // PIECES)
        return rcopy(b_ref.at[rows], bsib.at[rows], bss, bsr.at[i], sib)

    def send_a(u, k, w):
        return rcopy(p.at[u, k, ring(at1[k], 2), pl.ds(2 * w, 2)], ra.at[u, k, w], as_, ar.at[u], first[k][w])

    def send_b(u, k, w):
        return rcopy(p.at[u, k, ring(at1[k], HOPS[w]), pl.ds(2 - 2 * w, 2)], rbc.at[u, 0, k, w], bs_, bcr.at[u],
                     first[k][w])

    def send_c(u, k, w):
        return rcopy(m.at[u, k, w], rbc.at[u, 1, k, w], cs, bcr.at[u], first[k][w])

    def send_2(u, k, i):
        return rcopy(q.at[u, k, ring(at2[k], HOPS[i])], r2.at[u, k, i], st2s, st2r.at[u], second[k][i])

    def arrived(buf, sem):
        rcopy(buf, buf, ags.at[0], sem, up).wait_recv()

    def sent(buf, sem):
        rcopy(buf, buf, sem, agr.at[0, 0], up).wait_send()

    def zfar(u, h):
        return rcopy(red.at[u, h], zr.at[u, 0], zs, zrs.at[u], far[h])

    def zsib(u):
        return rcopy(red.at[u, 1 - c], zr.at[u, 1], zs, zrs.at[u], sib)

    PAIRS = [(k, w) for w in range(2) for k in range(2)]

    for s in range(AHEAD):
        for way in range(2):
            ag(s, way).start()
    for i in range(PIECES):
        bs(i).start()

    @pl.loop(0, T)
    def _(s):
        own_copy(s).start()

    def split(src, i, half):
        rows = pl.ds(pl.multiple_of(i * 128, 128), 128)
        v = src[rows, :]
        hi = v.astype(jnp.bfloat16)
        lo = (v - hi.astype(jnp.float32)).astype(jnp.bfloat16)
        cols = pl.ds(pl.multiple_of(half * K, K), K)
        bh[rows, cols] = hi
        bl[rows, cols] = lo

    def pass_on(s):
        for way in range(2):
            ag_in(s, way).wait_recv()
            fw(s, way).start()

    bcopy.wait()

    @pl.loop(0, K // 128)
    def _(i):
        split(bown, i, c)

    pass_on(0)

    for i in range(PIECES):
        bs(i).wait_recv()

    @pl.loop(0, K // 128)
    def _(i):
        split(bsib, i, 1 - c)

    def split_rows(s):
        a = apan[s].reshape(16 * R, K)
        hi = a.astype(jnp.bfloat16)
        both[: 16 * R] = hi
        both[16 * R :] = (a - hi.astype(jnp.float32)).astype(jnp.bfloat16)

    def multiply(u, i):
        for half in range(2):
            cols = pl.ds(pl.multiple_of(half * K + i * W, W), W)
            two = jnp.dot(both[...], bh[:, cols], preferred_element_type=jnp.float32)
            acc = jnp.dot(both[: 16 * R], bl[:, cols], preferred_element_type=jnp.float32)
            acc = (two[: 16 * R] + (two[16 * R :] + acc)).reshape(4, 4, R, W)
            if half == 0:
                p[u, 0] = acc
            else:
                for n in range(4):
                    p[u, 1, :, n] = acc[n]

    def exchange(u):
        @pl.when(zl == c)
        def _():
            zsib(u).start()

        @pl.when(zl != c)
        def _():
            for h in range(2):
                zfar(u, h).start()

    def finish(u):
        cols = pl.ds(pl.multiple_of((u % UN) * W, W), W)

        @pl.when(zl == c)
        def _():
            arrived(zr.at[u, 0], zrs.at[u])
            o_ref[u // UN, :, cols] = red[u, c] + zr[u, 0]

        @pl.when(zl != c)
        def _():
            arrived(zr.at[u], zrs.at[u])
            o_ref[u // UN, :, cols] = zr[u, 0] + zr[u, 1]

    @pl.loop(0, U + 4 * LAG)
    def _(u):
        i = u % UN
        s = u // UN

        @pl.when((i == 0) & (s < T))
        def _():
            @pl.when(s + AHEAD < T)
            def _():
                for way in range(2):
                    ag(s + AHEAD, way).start()

            @pl.when(s + 1 < T)
            def _():
                pass_on(s + 1)

            own_copy(s).wait()
            fw_in(s).wait_recv()
            split_rows(s)

        @pl.when(u == (T - 1) * UN)
        def _():
            @pl.loop(0, HELD)
            def _(t):
                exchange(t)

        @pl.when(u < U)
        def _():
            multiply(u, i)
            for k, w in PAIRS:
                send_a(u, k, w).start()
            for k, w in PAIRS:
                send_b(u, k, w).start()

        @pl.when((u >= LAG) & (u < U + LAG))
        def _():
            t = u - LAG
            arrived(ra.at[t], ar.at[t])
            for k, w in PAIRS:
                m[t, k, w] = p[t, k, ring(at1[k], HOPS[w]), 2 * w : 2 * w + 2] + ra[t, k, w]
                send_c(t, k, w).start()

        @pl.when((u >= 2 * LAG) & (u < U + 2 * LAG))
        def _():
            t = u - 2 * LAG
            arrived(rbc.at[t], bcr.at[t])
            for k in range(2):
                for w in range(2):
                    part = slice(2 * w, 2 * w + 2)
                    q[t, k, part] = p[t, k, at1[k], part] + (rbc[t, 0, k, 1 - w] + rbc[t, 1, k, w])
                for i2 in range(3):
                    send_2(t, k, i2).start()

        @pl.when(u == U - 1 + 2 * LAG)
        def _():
            @pl.loop(0, HELD)
            def _(t):
                finish(t)

        @pl.when((u >= 3 * LAG) & (u < U + 3 * LAG))
        def _():
            t = u - 3 * LAG
            arrived(r2.at[t], st2r.at[t])
            for k in range(2):
                red[t, k] = (q[t, k, at2[k]] + r2[t, k, 0]) + (r2[t, k, 1] + r2[t, k, 2])

            @pl.when(t >= HELD)
            def _():
                exchange(t)

        @pl.when(u >= HELD + 4 * LAG)
        def _():
            finish(u - 4 * LAG)

    sent(bsib, bss)
    for way in range(2):
        sent(apan.at[:, 0], ags.at[way])
        sent(apan.at[:, 0, pl.ds(0, 2)], fws.at[way])
    sent(ra, as_)
    sent(rbc.at[:, 0], bs_)
    sent(m, cs)
    sent(r2, st2s)

    @pl.when(zl == c)
    def _():
        sent(red.at[:, 0], zs)

    @pl.when(zl != c)
    def _():
        sent(red, zs)


def ladder(a, b):
    f32, bf16 = jnp.float32, jnp.bfloat16
    dma = pltpu.SemaphoreType.DMA
    return pl.pallas_call(
        kernel,
        out_shape=jax.ShapeDtypeStruct((T, R, K), f32),
        in_specs=[pl.BlockSpec(memory_space=pl.ANY)] * 2,
        out_specs=pl.BlockSpec(memory_space=pltpu.VMEM),
        scratch_shapes=[
            pltpu.VMEM((T, 4, 4, R, K), f32),
            pltpu.VMEM((K, K), f32),
            pltpu.VMEM((K, K), f32),
            pltpu.VMEM((K, 2 * K), bf16),
            pltpu.VMEM((K, 2 * K), bf16),
            pltpu.VMEM((32 * R, K), bf16),
            pltpu.VMEM((U, 2, 4, 4, R, W), f32),
            pltpu.VMEM((U, 2, 2, 2, R, W), f32),
            pltpu.VMEM((U, 2, 2, 2, 2, R, W), f32),
            pltpu.VMEM((U, 2, 2, 2, R, W), f32),
            pltpu.VMEM((U, 2, 4, R, W), f32),
            pltpu.VMEM((U, 2, 3, R, W), f32),
            pltpu.VMEM((U, 2, R, W), f32),
            pltpu.VMEM((U, 2, R, W), f32),
            dma((T,)), dma, dma, dma((PIECES,)),
            dma((2,)), dma((2, T)), dma((2,)), dma((T,)),
            dma, dma((U,)), dma, dma, dma((U,)), dma, dma((U,)), dma, dma((U,)),
        ],
        cost_estimate=pl.CostEstimate(flops=2 * 1152 * 2048 * 1024 * 3, bytes_accessed=8 * 2**20, transcendentals=0),
        compiler_params=pltpu.CompilerParams(collective_id=0, has_side_effects=True, vmem_limit_bytes=52 * 2**20),
    )(a, b)


def shards(amplitudes, integrals, residual_in):
    owned = ladder(amplitudes.reshape(4, T, R, K), integrals)
    return residual_in + owned.reshape(72, K)


def solution(mesh):
    placed = (P("cols", "depth"), P("depth", "cols"), P("depth", "cols"))
    return jax.shard_map(
        shards, mesh=mesh, in_specs=placed, out_specs=P("depth", "cols"), check_vma=False
    )
```

```python
import jax
import jax.numpy as jnp
from jax import lax
from jax.experimental import pallas as pl
from jax.experimental.pallas import tpu as pltpu
from jax.sharding import PartitionSpec as P

MESH = pl.DeviceIdType.MESH
K = 1024
R = 8
T = 72 // R
AHEAD = 2
UN = 2
W = K // UN
U = T * UN
LAG = 2
HELD = 4
PIECES = 4
HOPS = (1, -1, 2)


def kernel(a_ref, b_ref, o_ref, apan, bown, bsib, bh, bl, both, p, ra, rbc, m, q, r2, red, zr,
           own_sem, bown_sem, bss, bsr, ags, agr, fws, fwr, as_, ar, bs_, cs, bcr, st2s, st2r, zs, zrs):
    d = lax.axis_index("depth")
    j = lax.axis_index("cols")
    x, zl, y = d // 8, (d // 4) % 2, d % 4
    zh, c = j // 2, j % 2

    def dev(x_, zl_, y_, zh_, c_):
        return (x_ * 8 + zl_ * 4 + y_, zh_ * 2 + c_)

    def ring(v, n):
        return (v + n + 4) % 4

    up = dev(x, zl, y, ring(zh, 1), c)
    down = dev(x, zl, y, ring(zh, -1), c)
    sib = dev(x, zl, y, zh, 1 - c)
    xs = [dev(ring(x, n), zl, y, zh, c) for n in HOPS]
    ys = [dev(x, zl, ring(y, n), zh, c) for n in HOPS]
    far = [dev(x, 1 - zl, y, zh, h) for h in range(2)]
    opp = ring(zh, 2)
    first, second = (xs, ys), (ys, xs)
    at1, at2 = (x, y), (y, x)

    def rcopy(src, dst, ss, rs, to):
        return pltpu.make_async_remote_copy(
            src_ref=src, dst_ref=dst, send_sem=ss, recv_sem=rs, device_id=to, device_id_type=MESH
        )

    def own_copy(s):
        return pltpu.make_async_copy(a_ref.at[:, s], apan.at[s, zh], own_sem.at[s])

    bcopy = pltpu.make_async_copy(b_ref, bown, bown_sem)
    bcopy.start()

    peers = [up, down, sib] + xs + ys + far
    barrier = pltpu.get_barrier_semaphore()
    for peer in peers:
        pl.semaphore_signal(barrier, inc=1, device_id=peer, device_id_type=MESH)
    pl.semaphore_wait(barrier, len(peers))

    def ag(s, way):
        return rcopy(a_ref.at[:, s], apan.at[s, zh], ags.at[way], agr.at[way, s], (up, down)[way])

    def ag_in(s, way):
        blk = ring(zh, (-1, 1)[way])
        return rcopy(apan.at[s, blk], apan.at[s, blk], ags.at[way], agr.at[way, s], (up, down)[way])

    def fw(s, way):
        blk = ring(zh, (-1, 1)[way])
        part = pl.ds(2 * way, 2)
        return rcopy(apan.at[s, blk, part], apan.at[s, blk, part], fws.at[way], fwr.at[s],
                     (up, down)[way])

    def fw_in(s):
        return rcopy(apan.at[s, opp], apan.at[s, opp], fws.at[0], fwr.at[s], up)

    def bs(i):
        rows = pl.ds(i * (K // PIECES), K // PIECES)
        return rcopy(b_ref.at[rows], bsib.at[rows], bss, bsr.at[i], sib)

    def send_a(u, k, w):
        return rcopy(p.at[u, k, ring(at1[k], 2), pl.ds(2 * w, 2)], ra.at[u, k, w], as_, ar.at[u], first[k][w])

    def send_b(u, k, w):
        return rcopy(p.at[u, k, ring(at1[k], HOPS[w]), pl.ds(2 - 2 * w, 2)], rbc.at[u, 0, k, w], bs_, bcr.at[u],
                     first[k][w])

    def send_c(u, k, w):
        return rcopy(m.at[u, k, w], rbc.at[u, 1, k, w], cs, bcr.at[u], first[k][w])

    def send_2(u, k, i):
        return rcopy(q.at[u, k, ring(at2[k], HOPS[i])], r2.at[u, k, i], st2s, st2r.at[u], second[k][i])

    def arrived(buf, sem):
        rcopy(buf, buf, ags.at[0], sem, up).wait_recv()

    def sent(buf, sem):
        rcopy(buf, buf, sem, agr.at[0, 0], up).wait_send()

    def zfar(u, h):
        return rcopy(red.at[u, h], zr.at[u, 0], zs, zrs.at[u], far[h])

    def zsib(u):
        return rcopy(red.at[u, 1 - c], zr.at[u, 1], zs, zrs.at[u], sib)

    PAIRS = [(k, w) for w in range(2) for k in range(2)]

    for s in range(AHEAD):
        for way in range(2):
            ag(s, way).start()
    for i in range(PIECES):
        bs(i).start()

    @pl.loop(0, T)
    def _(s):
        own_copy(s).start()

    def split(src, i, half):
        rows = pl.ds(pl.multiple_of(i * 128, 128), 128)
        v = src[rows, :]
        hi = v.astype(jnp.bfloat16)
        lo = (v - hi.astype(jnp.float32)).astype(jnp.bfloat16)
        cols = pl.ds(pl.multiple_of(half * K, K), K)
        bh[rows, cols] = hi
        bl[rows, cols] = lo

    def pass_on(s):
        for way in range(2):
            ag_in(s, way).wait_recv()
            fw(s, way).start()

    bcopy.wait()

    @pl.loop(0, K // 128)
    def _(i):
        split(bown, i, c)

    pass_on(0)

    for i in range(PIECES):
        bs(i).wait_recv()

    @pl.loop(0, K // 128)
    def _(i):
        split(bsib, i, 1 - c)

    def split_rows(s):
        a = apan[s].reshape(16 * R, K)
        hi = a.astype(jnp.bfloat16)
        both[: 16 * R] = hi
        both[16 * R :] = (a - hi.astype(jnp.float32)).astype(jnp.bfloat16)

    def multiply(u, i):
        for half in range(2):
            cols = pl.ds(pl.multiple_of(half * K + i * W, W), W)
            two = jnp.dot(both[...], bh[:, cols], preferred_element_type=jnp.float32)
            acc = jnp.dot(both[: 16 * R], bl[:, cols], preferred_element_type=jnp.float32)
            acc = (two[: 16 * R] + (two[16 * R :] + acc)).reshape(4, 4, R, W)
            if half == 0:
                p[u, 0] = acc
            else:
                for n in range(4):
                    p[u, 1, :, n] = acc[n]

    def exchange(u):
        @pl.when(zl == c)
        def _():
            zsib(u).start()

        @pl.when(zl != c)
        def _():
            for h in range(2):
                zfar(u, h).start()

    def finish(u):
        cols = pl.ds(pl.multiple_of((u % UN) * W, W), W)

        @pl.when(zl == c)
        def _():
            arrived(zr.at[u, 0], zrs.at[u])
            o_ref[u // UN, :, cols] = red[u, c] + zr[u, 0]

        @pl.when(zl != c)
        def _():
            arrived(zr.at[u], zrs.at[u])
            o_ref[u // UN, :, cols] = zr[u, 0] + zr[u, 1]

    @pl.loop(0, U + 4 * LAG)
    def _(u):
        i = u % UN
        s = u // UN

        @pl.when((i == 0) & (s < T))
        def _():
            @pl.when(s + AHEAD < T)
            def _():
                for way in range(2):
                    ag(s + AHEAD, way).start()

            @pl.when(s + 1 < T)
            def _():
                pass_on(s + 1)

            own_copy(s).wait()
            fw_in(s).wait_recv()
            split_rows(s)

        @pl.when(u == (T - 1) * UN)
        def _():
            @pl.loop(0, HELD)
            def _(t):
                exchange(t)

        @pl.when(u < U)
        def _():
            multiply(u, i)
            for k, w in PAIRS:
                send_a(u, k, w).start()
            for k, w in PAIRS:
                send_b(u, k, w).start()

        @pl.when((u >= LAG) & (u < U + LAG))
        def _():
            t = u - LAG
            arrived(ra.at[t], ar.at[t])
            for k, w in PAIRS:
                m[t, k, w] = p[t, k, ring(at1[k], HOPS[w]), 2 * w : 2 * w + 2] + ra[t, k, w]
                send_c(t, k, w).start()

        @pl.when((u >= 2 * LAG) & (u < U + 2 * LAG))
        def _():
            t = u - 2 * LAG
            arrived(rbc.at[t], bcr.at[t])
            for k in range(2):
                for w in range(2):
                    part = slice(2 * w, 2 * w + 2)
                    q[t, k, part] = p[t, k, at1[k], part] + (rbc[t, 0, k, 1 - w] + rbc[t, 1, k, w])
                for i2 in range(3):
                    send_2(t, k, i2).start()

        @pl.when(u == U - 1 + 2 * LAG)
        def _():
            @pl.loop(0, HELD)
            def _(t):
                finish(t)

        @pl.when((u >= 3 * LAG) & (u < U + 3 * LAG))
        def _():
            t = u - 3 * LAG
            arrived(r2.at[t], st2r.at[t])
            for k in range(2):
                red[t, k] = (q[t, k, at2[k]] + r2[t, k, 0]) + (r2[t, k, 1] + r2[t, k, 2])

            @pl.when(t >= HELD)
            def _():
                exchange(t)

        @pl.when(u >= HELD + 4 * LAG)
        def _():
            finish(u - 4 * LAG)

    sent(bsib, bss)
    for way in range(2):
        sent(apan.at[:, 0], ags.at[way])
        sent(apan.at[:, 0, pl.ds(0, 2)], fws.at[way])
    sent(ra, as_)
    sent(rbc.at[:, 0], bs_)
    sent(m, cs)
    sent(r2, st2s)

    @pl.when(zl == c)
    def _():
        sent(red.at[:, 0], zs)

    @pl.when(zl != c)
    def _():
        sent(red, zs)


def ladder(a, b):
    f32, bf16 = jnp.float32, jnp.bfloat16
    dma = pltpu.SemaphoreType.DMA
    return pl.pallas_call(
        kernel,
        out_shape=jax.ShapeDtypeStruct((T, R, K), f32),
        in_specs=[pl.BlockSpec(memory_space=pl.ANY)] * 2,
        out_specs=pl.BlockSpec(memory_space=pltpu.VMEM),
        scratch_shapes=[
            pltpu.VMEM((T, 4, 4, R, K), f32),
            pltpu.VMEM((K, K), f32),
            pltpu.VMEM((K, K), f32),
            pltpu.VMEM((K, 2 * K), bf16),
            pltpu.VMEM((K, 2 * K), bf16),
            pltpu.VMEM((32 * R, K), bf16),
            pltpu.VMEM((U, 2, 4, 4, R, W), f32),
            pltpu.VMEM((U, 2, 2, 2, R, W), f32),
            pltpu.VMEM((U, 2, 2, 2, 2, R, W), f32),
            pltpu.VMEM((U, 2, 2, 2, R, W), f32),
            pltpu.VMEM((U, 2, 4, R, W), f32),
            pltpu.VMEM((U, 2, 3, R, W), f32),
            pltpu.VMEM((U, 2, R, W), f32),
            pltpu.VMEM((U, 2, R, W), f32),
            dma((T,)), dma, dma, dma((PIECES,)),
            dma((2,)), dma((2, T)), dma((2,)), dma((T,)),
            dma, dma((U,)), dma, dma, dma((U,)), dma, dma((U,)), dma, dma((U,)),
        ],
        cost_estimate=pl.CostEstimate(flops=2 * 1152 * 2048 * 1024 * 3, bytes_accessed=8 * 2**20, transcendentals=0),
        compiler_params=pltpu.CompilerParams(collective_id=0, has_side_effects=True, vmem_limit_bytes=52 * 2**20),
    )(pltpu.with_memory_space_constraint(a, pltpu.HBM), b)


def shards(amplitudes, integrals, residual_in):
    owned = ladder(amplitudes.reshape(4, T, R, K), integrals)
    return residual_in + owned.reshape(72, K)


def solution(mesh):
    placed = (P("cols", "depth"), P("depth", "cols"), P("depth", "cols"))
    return jax.shard_map(
        shards, mesh=mesh, in_specs=placed, out_specs=P("depth", "cols"), check_vma=False
    )
```
